32 devices in a mesh: copies: 2 (over x), expert: 4 (over y, core), tm: 4 (over z).
Axes of the slice: x: 2, y: 2, z: 4, core: 2. Of those that a mesh axis runs over, the one named last changes fastest.
Arguments:
- tokens: bfloat16 [4, 1024, 2048], P('tm', ('copies', 'expert')), parts along dimension 1, may hold values from -6 to 6
- route_ids: int32 [4, 1024, 6], P('tm', ('copies', 'expert')), parts along dimension 1, may hold values from 0 to 15, all different within a row; in each aligned block of 128 rows (0 to 127, 128 to 255, ..., all dimensions but the last counted through in order) at most 72 rows name the same one
- route_probs: float32 [4, 1024, 6], P('tm', ('copies', 'expert')), parts along dimension 1, may hold values from 0.05 to 1
- step_size: float32 [8], P(('copies', 'tm')), parts along dimension 0, may hold values from 0.2 to 0.6
- start_state: float32 [1024, 2048], P(('copies', 'expert')), parts along dimension 0, may hold values from -6 to 6
- w_gate: bfloat16 [16, 2048, 768], P('expert'), may hold values from -0.125 to 0.125
- w_up: bfloat16 [16, 2048, 768], P('expert'), may hold values from -0.125 to 0.125
- w_down: bfloat16 [16, 768, 2048], P('expert'), may hold values from -0.21875 to 0.21875
Outputs:
- new_iterate: float32 [4, 1024, 2048], P('tm', ('copies', 'expert')), parts along dimension 1
The draws below stay inside these ranges and needn't reach their ends.
There are 2 independent parts, one for each index of `copies`. The reference program is written for one: setup_inputs(seed, part) draws one part's arguments, and reference() takes and returns one part's arrays. A program takes and returns all parts, laid end to end along the dimension named above; an argument that names none is the same for every part. Nothing has to cross between parts.
Inputs may be any that keep to these rules, and one draw needn't show every extreme that they name: `route_ids`: each row names 6 different experts. In each aligned block of 128 rows (the tokens of one device), no expert is named by more than 72 rows, a bound that some block reaches.
All inputs are finite; a program needn't handle non-finite values.
Results may differ from the reference program's by a relative error of at most 0.0018.
Values may be sent and summed in bfloat16 or wider, within the bound.
A program may use at most 128 MiB of HBM per device.

```python
import math
import jax
import jax.numpy as jnp
import numpy as np
from jax import lax

D = 2048
FF = 768
TOPK = 6
TOK_DEV = 128
EXPERTS = 16
C = 72
TIMESTEPS = 4
GROUP_TOK = 512
N_EXPERT = 4


def levels(rng, extent, pieces, smallest, largest):
    def one(dim, parts):
        draws = jax.random.uniform(jax.random.fold_in(jax.random.fold_in(rng, 6), dim), (parts,), jnp.float32, smallest / len(pieces), largest / len(pieces))
        return jnp.repeat(jnp.exp(draws), extent[dim] // parts).reshape((-1,) + (1,) * (len(extent) - dim - 1))

    factor_of = one(*pieces[0])
    for cut in pieces[1:]:
        factor_of = factor_of * one(*cut)
    return factor_of


def assign_block(rng, own, number, rows, count, top, reach, skew):
    order = jax.random.permutation(rng, count)
    packed, ordinary = load_shares(count, rows * top, reach, skew, True), load_shares(count, rows * top, reach, skew, False)
    places = jnp.arange(count)

    def named(lengths, rotation):
        used = int((lengths > 0).sum())
        fixed = max(1, used // 4)
        shifted = fixed + (places - fixed + rotation * (used - fixed)) % max(1, count - fixed)
        return jnp.zeros((count,), jnp.int32).at[order[jnp.where(places < fixed, places, shifted)]].set(jnp.asarray(lengths, jnp.int32))

    lengths = jnp.where(number % 4 == 0, named(packed, number // 4), named(ordinary, number - number // 4 - 1))
    mixed = jax.random.permutation(jax.random.fold_in(own, 3), count)
    donor, receiver = mixed[0:count // 2 * 2:2], mixed[1:count // 2 * 2:2]
    margin = jnp.minimum(lengths[donor] - 1, reach - lengths[receiver]) // 2
    margin = jnp.where((donor == order[0]) | (receiver == order[0]) | (lengths[receiver] == 0), 0, jnp.maximum(margin, 0))
    shifted = jax.random.randint(jax.random.fold_in(own, 4), (count // 2,), 0, 1 << 20) % (margin + 1)
    lengths = lengths.at[donor].add(-shifted).at[receiver].add(shifted)
    labels = jnp.searchsorted(jnp.cumsum(lengths), jnp.arange(rows * top), side="right").astype(jnp.int32)
    listing = labels.reshape(top, rows).T
    listing = listing[jax.random.permutation(jax.random.fold_in(own, 1), rows)]
    rotation = jax.random.randint(jax.random.fold_in(own, 2), (rows, 1), 0, top)
    return jnp.take_along_axis(listing, (jnp.arange(top)[None, :] + rotation) % top, axis=1)


def load_shares(amount, total, reach, slope, full):
    portions = [(1 << 20) // math.isqrt(rank ** slope) + 1 for rank in range(1, amount + 1)]
    largest = reach if full else min(reach, max(-(-total // amount), total * portions[0] // sum(portions)))
    least = 1 if total - largest >= amount - 1 else 0
    counts, spare = [largest] + [least] * (amount - 1), total - largest - least * (amount - 1)
    while spare > 0:
        movable = [i for i in range(1, amount) if counts[i] < largest] or [i for i in range(1, amount) if counts[i] < reach]
        whole, budget = sum([portions[i] for i in movable]), spare
        for i in movable:
            addition = min(reach - counts[i], max(1, budget * portions[i] // whole), spare)
            counts[i] = counts[i] + addition
            spare = spare - addition
    return np.array(counts)


def bell_draw(own_key, extent, spread, bound, split=(), kind=jnp.bfloat16):
    drawn = spread * jax.random.normal(own_key, extent, jnp.float32)
    if split:
        drawn = drawn * levels(own_key, extent, split, -0.22, 0.18)
    return jnp.clip(drawn, -bound, bound).astype(kind)


def setup_inputs(seed: int = 0, part: int = 0) -> dict:
    keys = jax.random.split(jax.random.key(seed), 9)
    part_keys = jax.random.split(jax.random.fold_in(keys[8], part), 9)
    tokens = bell_draw(part_keys[0], (TIMESTEPS, GROUP_TOK, D), 1.0, 6.0, ((0, 4), (1, 4)))
    route_ids_keys = jax.random.split(jax.random.fold_in(part_keys[1], 1), TIMESTEPS * GROUP_TOK // TOK_DEV)
    route_ids_turns = jax.random.permutation(jax.random.fold_in(part_keys[1], 3), TIMESTEPS * GROUP_TOK // TOK_DEV)
    route_ids = jax.vmap(lambda own, number: assign_block(jax.random.fold_in(part_keys[1], 2), own, number, TOK_DEV, EXPERTS, TOPK, C, 2))(route_ids_keys, route_ids_turns).reshape((TIMESTEPS, GROUP_TOK, TOPK))
    route_probs = jnp.clip(0.05 + 0.95 * jax.random.uniform(part_keys[2], (TIMESTEPS, GROUP_TOK, TOPK), jnp.float32) ** levels(part_keys[2], (TIMESTEPS, GROUP_TOK, TOPK), ((0, 4), (1, 4)), -0.2, 0.2), 0.05, 1.0)
    step_size = jnp.clip(jnp.exp(math.log(0.6) - 1.0986123 * jax.random.uniform(part_keys[3], (TIMESTEPS,), jnp.float32) ** levels(part_keys[3], (TIMESTEPS,), ((0, 4),), -0.2, 0.2)), 0.2, 0.6)
    start_state = bell_draw(part_keys[4], (GROUP_TOK, D), 1.0, 6.0, ((0, 4),), jnp.float32)
    w_gate = bell_draw(keys[5], (EXPERTS, D, FF), D ** -0.5, 0.125, ((0, 4),))
    w_up = bell_draw(keys[6], (EXPERTS, D, FF), D ** -0.5, 0.125, ((0, 4),))
    w_down = bell_draw(keys[7], (EXPERTS, FF, D), FF ** -0.5, 0.21875, ((0, 4),))
    return {"tokens": tokens, "route_ids": route_ids, "route_probs": route_probs, "step_size": step_size, "start_state": start_state, "w_gate": w_gate, "w_up": w_up, "w_down": w_down}


def reference(tokens, route_ids, route_probs, step_size, start_state, w_gate, w_up, w_down):
    blocks = TIMESTEPS * N_EXPERT
    values = tokens.astype(jnp.float32)
    normed = (values * lax.rsqrt(lax.optimization_barrier(jnp.mean(values * values, axis=-1, keepdims=True)) + 1e-06)).astype(jnp.bfloat16)
    normed = normed.reshape(blocks, TOK_DEV, D)
    padded = jnp.concatenate([normed, jnp.zeros((blocks, 1, D), jnp.bfloat16)], axis=1)
    flat_ids = route_ids.reshape(blocks, TOK_DEV * TOPK).astype(jnp.int32)
    one_hot = (flat_ids[:, :, None] == jnp.arange(EXPERTS, dtype=jnp.int32)[None, None, :]).astype(jnp.int32)
    earlier = jnp.cumsum(one_hot, axis=1) - one_hot
    position = lax.optimization_barrier(jnp.sum(earlier * one_hot, axis=2)).astype(jnp.int32)
    slot_index = (flat_ids * C + position).astype(jnp.int32)
    gate_probs = route_probs.astype(jnp.float32)
    weights = (gate_probs / lax.optimization_barrier(jnp.sum(gate_probs, axis=-1, keepdims=True))).reshape(blocks, TOK_DEV * TOPK)
    block_ids = jnp.arange(blocks, dtype=jnp.int32)[:, None]
    token_of = jnp.broadcast_to((jnp.arange(TOK_DEV * TOPK, dtype=jnp.int32) // TOPK)[None, :], slot_index.shape)
    slot_table = jnp.full((blocks, EXPERTS * C), TOK_DEV, jnp.int32).at[block_ids, slot_index].set(token_of)
    weight_table = jnp.zeros((blocks, EXPERTS * C), jnp.float32).at[block_ids, slot_index].set(weights)

    def expert_step(drift_rows, operands):
        gate_one, up_one, down_one, expert = operands
        slot_tokens = lax.dynamic_slice_in_dim(slot_table, expert * C, C, 1)
        scales = lax.dynamic_slice_in_dim(weight_table, expert * C, C, 1)
        slot_rows = jnp.take_along_axis(padded, slot_tokens[:, :, None], axis=1).reshape(blocks * C, D)
        gate_act = jnp.dot(slot_rows, gate_one, preferred_element_type=jnp.float32)
        up_act = jnp.dot(slot_rows, up_one, preferred_element_type=jnp.float32)
        hidden = (jax.nn.silu(gate_act) * up_act).astype(jnp.bfloat16)
        result = jnp.dot(hidden, down_one, preferred_element_type=jnp.float32).astype(jnp.bfloat16)
        result = lax.optimization_barrier(result).astype(jnp.float32).reshape(blocks, C, D)
        drift_rows = drift_rows.at[block_ids, slot_tokens].add(scales[:, :, None] * result)
        return (drift_rows, None)
    initial = jnp.zeros((blocks, TOK_DEV + 1, D), jnp.float32)
    drift_rows, unused_out = lax.scan(expert_step, initial, (w_gate, w_up, w_down, jnp.arange(EXPERTS, dtype=jnp.int32)))
    drift_rows = drift_rows[:, :TOK_DEV, :].reshape(TIMESTEPS, GROUP_TOK, D)
    increment = step_size.astype(jnp.float32)[:, None, None] * drift_rows
    return start_state[None, :, :] + jnp.cumsum(increment, axis=0)
```

```python
import functools

import jax
import jax.numpy as jnp
from jax import lax
from jax.experimental import pallas as pl
from jax.experimental.pallas import tpu as pltpu
from jax.sharding import PartitionSpec as P

MESH = pl.DeviceIdType.MESH
BF16 = jnp.bfloat16
F32 = jnp.float32
PARTS = 2
FT = 256
DC = 256
META = 16


def fit(total, wanted):
    return wanted if total % wanted == 0 else total


def kernel(
    dims,
    tok_in, meta_in, start_in, wg_hbm, wu_hbm, wd_hbm, out_ref,
    wg, wu, wd, tok, meta, xn, pos, wt, rows, hid, mmap, ycat,
    keep, px_out, px_in, y_out, y_in, z_out, z_in,
    w_sem, t_send, f_send, t_recv, m_send, m_recv,
    px_send, px_recv, y_send, y_recv, z_send, z_recv,
):
    chips, steps, cap, slots = dims
    local, width, ff = wg.shape
    toks = tok_in.shape[0]
    chunks = keep.shape[1]
    dc = keep.shape[3]
    ft = fit(ff, FT)
    part = toks // PARTS
    me = lax.axis_index("expert")
    now = lax.axis_index("tm")
    core = lax.rem(me, 2)
    chip = lax.div(me, 2)

    def peer(offset, other):
        own = (1 - core) if other else core
        return {"expert": lax.rem(chip + offset, chips) * 2 + own}

    def remote(src, dst, send, recv, where):
        return pltpu.make_async_remote_copy(
            src_ref=src, dst_ref=dst, send_sem=send, recv_sem=recv,
            device_id=where, device_id_type=MESH,
        )

    def weight_copy(kind, e):
        src, dst = ((wg_hbm, wg), (wu_hbm, wu), (wd_hbm, wd))[kind]
        return pltpu.make_async_copy(src.at[e], dst.at[e], w_sem.at[kind, e])

    for e in range(local):
        for kind in range(2):
            weight_copy(kind, e).start()
    for e in range(local):
        weight_copy(2, e).start()

    barrier = pltpu.get_barrier_semaphore()
    for d in range(chips):
        for other in (False, True):
            if d or other:
                pl.semaphore_signal(barrier, inc=1, device_id=peer(d, other), device_id_type=MESH)

    @pl.when(now > 0)
    def _():
        pl.semaphore_signal(barrier, inc=1, device_id={"tm": now - 1}, device_id_type=MESH)

    @pl.when(now < steps - 1)
    def _():
        pl.semaphore_signal(barrier, inc=1, device_id={"tm": now + 1}, device_id_type=MESH)

    peers = 2 * chips - 1 + jnp.where(now > 0, 1, 0) + jnp.where(now < steps - 1, 1, 0)
    pl.semaphore_wait(barrier, peers)

    def tok_copy(d, q):
        span = pl.ds(q * part, part)
        slot, side = ((chips - d) % chips, 0) if d else (0, 1)
        return remote(
            tok_in.at[span], tok.at[slot, side, span], t_send.at[d, q],
            t_recv.at[slot, side, q], peer(d, d == 0),
        )

    def meta_copy(d, other):
        slot, side = (chips - d) % chips, int(other)
        return remote(
            meta_in, meta.at[slot, side], m_send.at[d, side], m_recv.at[slot, side], peer(d, other)
        )

    def forward_copy(j, q):
        span = pl.ds(q * part, part)
        return remote(
            tok.at[j, 0, span], tok.at[j, 1, span], f_send.at[j, q], t_recv.at[j, 1, q],
            peer(0, True),
        )

    def tok_arrival(j, side, q):
        span = pl.ds(q * part, part)
        return remote(
            tok.at[j, side, span], tok.at[j, side, span], f_send.at[j, q],
            t_recv.at[j, side, q], peer(0, True),
        )

    def meta_arrival(j, side):
        return remote(
            meta_in, meta.at[j, side], m_send.at[0, 1], m_recv.at[j, side], peer(0, True)
        )

    meta_copy(0, True).start()
    for q in range(PARTS):
        tok_copy(0, q).start()
    for d in range(1, chips):
        for other in (False, True):
            meta_copy(d, other).start()
        for q in range(PARTS):
            tok_copy(d, q).start()

    def place(values, j, side):
        rows8 = pos.shape[2]
        names = (me * local + lax.broadcasted_iota(jnp.int32, (rows8, toks), 0)).astype(F32)
        member = jnp.zeros((rows8, toks), F32)
        weight = jnp.zeros((rows8, toks), F32)
        half = META // 2
        for k in range(half):
            hit = values[k : k + 1, :] == names
            member = member + jnp.where(hit, 1.0, 0.0)
            weight = weight + jnp.where(hit, values[half + k : half + k + 1, :], 0.0)
        earlier = (
            lax.broadcasted_iota(jnp.int32, (toks, toks), 0)
            < lax.broadcasted_iota(jnp.int32, (toks, toks), 1)
        )
        count = jnp.dot(
            member.astype(BF16), jnp.where(earlier, 1.0, 0.0).astype(BF16),
            preferred_element_type=F32,
        )
        pos[j, side] = jnp.where(member > 0.0, count, -4096.0)
        wt[j, side] = weight

    def normalise(src, j, side):
        group = 16

        def one(i, carry):
            span = pl.ds(pl.multiple_of(i * group, group), group)
            values = src[span, :].astype(F32)
            mean = jnp.mean(values * values, axis=-1, keepdims=True)
            into = pl.ds(pl.multiple_of(side * toks + i * group, group), group)
            xn[j, into, :] = (values * lax.rsqrt(mean + 1e-06)).astype(BF16)
            return carry

        lax.fori_loop(0, toks // group, one, 0)

    def gate_up(j, hs, first):
        rid = lax.broadcasted_iota(jnp.int32, (slots, toks), 0).astype(F32)

        def per_expert(e, carry):
            if first:
                for kind in range(2):
                    weight_copy(kind, e).wait()
            near = rid == pos[j, 0, pl.ds(e, 1), :]
            far = (rid - cap) == pos[j, 1, pl.ds(e, 1), :]
            chosen = jnp.concatenate(
                [jnp.where(near, 1.0, 0.0), jnp.where(far, 1.0, 0.0)], axis=1
            ).astype(BF16)
            scale = jnp.sum(
                jnp.where(near, wt[j, 0, pl.ds(e, 1), :], 0.0)
                + jnp.where(far, wt[j, 1, pl.ds(e, 1), :], 0.0),
                axis=1, keepdims=True,
            )
            mmap[hs, pl.ds(pl.multiple_of(e * slots, 16), slots), :] = chosen
            wide = fit(width, 512)

            def pick(i, c2):
                cols = pl.ds(pl.multiple_of(i * wide, 128), wide)
                rows[:, cols] = jnp.dot(
                    chosen, xn[j, :, cols], preferred_element_type=F32
                ).astype(BF16)
                return c2

            lax.fori_loop(0, width // wide, pick, 0)

            def tile(i, c2):
                cols = pl.ds(pl.multiple_of(i * ft, 128), ft)
                gate = jnp.dot(rows[...], wg[e, :, cols], preferred_element_type=F32)
                up = jnp.dot(rows[...], wu[e, :, cols], preferred_element_type=F32)
                hid[hs, e, :, cols] = (
                    gate / (1.0 + jnp.exp(-gate)) * up * scale
                ).astype(BF16)
                return c2

            lax.fori_loop(0, ff // ft, tile, 0)
            return carry

        lax.fori_loop(0, local, per_expert, 0)

    def pair_copy(j, k):
        return remote(
            px_out.at[j, k], px_in.at[j, k], px_send.at[j, k], px_recv.at[j, k], peer(0, True)
        )

    def back_copy(j, k):
        slot = chips - j
        return remote(
            y_out.at[j, k], y_in.at[slot, k], y_send.at[j, k], y_recv.at[slot, k], peer(j, False)
        )

    def rise_copy(k):
        return remote(
            z_out.at[k], z_in.at[k], z_send.at[k], z_recv.at[k], {"tm": lax.rem(now + 1, steps)}
        )

    def down(j, hs, k):
        cols = pl.ds(pl.multiple_of(k * dc, 128), dc)
        for e in range(local):
            ycat[e * slots : (e + 1) * slots, :] = jnp.dot(
                hid[hs, e], wd[e, :, cols], preferred_element_type=F32
            ).astype(BF16)
        share = lax.dot_general(
            mmap[hs], ycat[...], (((0,), (0,)), ((), ())), preferred_element_type=F32
        )
        px_out[j, k] = share[toks:].astype(BF16)
        keep[hs, k] = share[:toks]
        pair_copy(j, k).start()

    def send_back(j, k):
        pair_copy(j, k).wait_recv()
        y_out[j, k] = (keep[1, k] + px_in[j, k].astype(F32)).astype(BF16)
        back_copy(j, k).start()

    place(meta_in[...], 0, 0)
    normalise(tok_in, 0, 0)
    meta_arrival(0, 1).wait_recv()
    place(meta[0, 1], 0, 1)
    for q in range(PARTS):
        tok_arrival(0, 1, q).wait_recv()
    normalise(tok.at[0, 1], 0, 1)
    gate_up(0, 0, True)

    def far_chip(j, carry):
        for q in range(PARTS):
            tok_arrival(j, 0, q).wait_recv()
            forward_copy(j, q).start()
        for side in range(2):
            meta_arrival(j, side).wait_recv()
            place(meta[j, side], j, side)
        normalise(tok.at[j, 0], j, 0)
        for q in range(PARTS):
            tok_arrival(j, 1, q).wait_recv()
        normalise(tok.at[j, 1], j, 1)
        gate_up(j, 1, False)

        @pl.when(j == 1)
        def _():
            for e in range(local):
                weight_copy(2, e).wait()

        down(j, 1, 0)

        def step(k, c2):
            down(j, 1, k)
            send_back(j, k - 1)
            return c2

        lax.fori_loop(1, chunks, step, 0)
        send_back(j, chunks - 1)
        return carry

    lax.fori_loop(1, chips, far_chip, 0)

    if chips == 1:
        for e in range(local):
            weight_copy(2, e).wait()

    def own(k, carry):
        down(0, 0, k)
        return carry

    lax.fori_loop(0, chunks, own, 0)

    def finish(k, carry):
        cols = pl.ds(pl.multiple_of(k * dc, 128), dc)
        pair_copy(0, k).wait_recv()
        total = keep[0, k] + px_in[0, k].astype(F32)
        for j in range(1, chips):
            back_copy(chips - j, k).wait_recv()
            total = total + y_in[j, k].astype(F32)
        keep[0, k] = total

        @pl.when(now > 0)
        def _():
            rise_copy(k).wait_recv()
            keep[0, k] = keep[0, k] + z_in[k].astype(F32)

        @pl.when(now < steps - 1)
        def _():
            z_out[k] = keep[0, k].astype(BF16)
            rise_copy(k).start()

        out_ref[:, cols] = start_in[:, cols] + keep[0, k]
        return carry

    lax.fori_loop(0, chunks, finish, 0)

    meta_copy(0, True).wait_send()
    for q in range(PARTS):
        tok_copy(0, q).wait_send()
    for d in range(1, chips):
        for other in (False, True):
            meta_copy(d, other).wait_send()
        for q in range(PARTS):
            tok_copy(d, q).wait_send()
            forward_copy(d, q).wait_send()

    def drain(k, carry):
        for j in range(chips):
            pair_copy(j, k).wait_send()
            if j:
                back_copy(j, k).wait_send()

        @pl.when(now < steps - 1)
        def _():
            rise_copy(k).wait_send()

        return carry

    lax.fori_loop(0, chunks, drain, 0)


def shards(mesh, tokens, route_ids, route_probs, step_size, start_state, w_gate, w_up, w_down):
    toks, width = tokens.shape[1:]
    topk = route_ids.shape[2]
    local, _, ff = w_gate.shape
    group = mesh.shape["expert"]
    steps = mesh.shape["tm"]
    chips = group // 2
    cap = 3 * toks * topk // (2 * local * group)
    slots = -(-2 * cap // 16) * 16
    dc = fit(width, DC)
    chunks = width // dc
    half = META // 2
    local8 = -(-local // 8) * 8

    probs = route_probs[0]
    weights = step_size[0] * probs / jnp.sum(probs, axis=-1, keepdims=True)
    names = jnp.pad(route_ids[0].astype(F32), ((0, 0), (0, half - topk)), constant_values=-1.0)
    weights = jnp.pad(weights, ((0, 0), (0, half - topk)))
    meta = jnp.concatenate([names, weights], axis=1).T

    vmem = pl.BlockSpec(memory_space=pltpu.VMEM)
    hbm = pl.BlockSpec(memory_space=pl.ANY)
    dma = pltpu.SemaphoreType.DMA
    out = pl.pallas_call(
        functools.partial(kernel, (chips, steps, cap, slots)),
        out_shape=jax.ShapeDtypeStruct((toks, width), F32),
        in_specs=[vmem, vmem, vmem, hbm, hbm, hbm],
        out_specs=vmem,
        scratch_shapes=[
            pltpu.VMEM((local, width, ff), BF16),
            pltpu.VMEM((local, width, ff), BF16),
            pltpu.VMEM((local, ff, width), BF16),
            pltpu.VMEM((chips, 2, toks, width), BF16),
            pltpu.VMEM((chips, 2, META, toks), F32),
            pltpu.VMEM((chips, 2 * toks, width), BF16),
            pltpu.VMEM((chips, 2, local8, toks), F32),
            pltpu.VMEM((chips, 2, local8, toks), F32),
            pltpu.VMEM((slots, width), BF16),
            pltpu.VMEM((2, local, slots, ff), BF16),
            pltpu.VMEM((2, local * slots, 2 * toks), BF16),
            pltpu.VMEM((local * slots, dc), BF16),
            pltpu.VMEM((2, chunks, toks, dc), F32),
            pltpu.VMEM((chips, chunks, toks, dc), BF16),
            pltpu.VMEM((chips, chunks, toks, dc), BF16),
            pltpu.VMEM((chips, chunks, toks, dc), BF16),
            pltpu.VMEM((chips, chunks, toks, dc), BF16),
            pltpu.VMEM((chunks, toks, dc), BF16),
            pltpu.VMEM((chunks, toks, dc), BF16),
            dma((3, local)),
            dma((chips, PARTS)),
            dma((chips, PARTS)),
            dma((chips, 2, PARTS)),
            dma((chips, 2)),
            dma((chips, 2)),
            dma((chips, chunks)),
            dma((chips, chunks)),
            dma((chips, chunks)),
            dma((chips, chunks)),
            dma((chunks,)),
            dma((chunks,)),
        ],
        compiler_params=pltpu.CompilerParams(
            collective_id=0, has_side_effects=True, vmem_limit_bytes=67_043_328
        ),
    )(tokens[0], meta, start_state, w_gate, w_up, w_down)
    return out[None]


def solution(mesh):
    return jax.shard_map(
        functools.partial(shards, mesh),
        mesh=mesh,
        in_specs=(
            P("tm", ("copies", "expert"), None),
            P("tm", ("copies", "expert"), None),
            P("tm", ("copies", "expert"), None),
            P(("copies", "tm")),
            P(("copies", "expert"), None),
            P("expert", None, None),
            P("expert", None, None),
            P("expert", None, None),
        ),
        out_specs=P("tm", ("copies", "expert"), None),
        check_vma=False,
    )
```

```python
import functools

import jax
import jax.numpy as jnp
from jax import lax
from jax.experimental import pallas as pl
from jax.experimental.pallas import tpu as pltpu
from jax.sharding import PartitionSpec as P

MESH = pl.DeviceIdType.MESH
BF16 = jnp.bfloat16
F32 = jnp.float32
COLS = 512
FT = 384
DC = 256


def fit(total, wanted):
    return wanted if total % wanted == 0 else total


def kernel(
    dims,
    tok_in, ids_in, probs_in, step_in, wg_hbm, wu_hbm, wd_hbm, out_ref,
    wg, wu, wd, tok, ids, probs, scale, squares, rows, acc_g, acc_u, hid, mmap, ycat,
    keep, px_out, px_in, y_out, y_in, z_out, z_in,
    up_sem, down_sem, t_send, f_send, t_recv, i_send, i_recv, p_send, p_recv,
    px_send, px_recv, y_send, y_recv, z_send, z_recv,
):
    chips, steps, cap, slots = dims
    local, width, ff = wg.shape
    toks = tok_in.shape[0]
    topk = ids_in.shape[0]
    parts, cq = tok.shape[1], tok.shape[3]
    chunks, dc = keep.shape[1], keep.shape[3]
    ft = fit(ff, FT)
    me = lax.axis_index("expert")
    now = lax.axis_index("tm")
    core = lax.rem(me, 2)
    chip = lax.div(me, 2)

    def peer(offset, other):
        own = (1 - core) if other else core
        return {"expert": lax.rem(chip + offset, chips) * 2 + own}

    def remote(src, dst, send, recv, where):
        return pltpu.make_async_remote_copy(
            src_ref=src, dst_ref=dst, send_sem=send, recv_sem=recv,
            device_id=where, device_id_type=MESH,
        )

    def up_copy(kind, e, q):
        src, dst = ((wg_hbm, wg), (wu_hbm, wu))[kind]
        span = pl.ds(pl.multiple_of(q * cq, 128), cq)
        return pltpu.make_async_copy(src.at[e, span], dst.at[e, span], up_sem.at[kind, e, q])

    def down_copy(e):
        return pltpu.make_async_copy(wd_hbm.at[e], wd.at[e], down_sem.at[e])

    for q in range(parts):
        for e in range(local):
            for kind in range(2):
                up_copy(kind, e, q).start()
    for e in range(local):
        down_copy(e).start()

    barrier = pltpu.get_barrier_semaphore()
    for d in range(chips):
        for other in (False, True):
            if d or other:
                pl.semaphore_signal(barrier, inc=1, device_id=peer(d, other), device_id_type=MESH)

    @pl.when(now > 0)
    def _():
        pl.semaphore_signal(barrier, inc=1, device_id={"tm": now - 1}, device_id_type=MESH)

    @pl.when(now < steps - 1)
    def _():
        pl.semaphore_signal(barrier, inc=1, device_id={"tm": now + 1}, device_id_type=MESH)

    peers = 2 * chips - 1 + jnp.where(now > 0, 1, 0) + jnp.where(now < steps - 1, 1, 0)
    pl.semaphore_wait(barrier, peers)

    def tok_copy(d, q):
        slot, side = ((chips - d) % chips, 0) if d else (0, 1)
        return remote(
            tok_in.at[:, pl.ds(q * cq, cq)], tok.at[slot, q, pl.ds(side * toks, toks)],
            t_send.at[d, q], t_recv.at[slot, side, q], peer(d, d == 0),
        )

    def route_copies(d, other):
        slot, side = (chips - d) % chips, int(other)
        where = peer(d, other)
        return (
            remote(ids_in, ids.at[slot, side], i_send.at[d, side], i_recv.at[slot, side], where),
            remote(
                probs_in, probs.at[slot, side], p_send.at[d, side], p_recv.at[slot, side], where
            ),
        )

    def forward_copy(j, q):
        return remote(
            tok.at[j, q, pl.ds(0, toks)], tok.at[j, q, pl.ds(toks, toks)],
            f_send.at[j, q], t_recv.at[j, 1, q], peer(0, True),
        )

    def tok_arrival(j, side, q):
        span = tok.at[j, q, pl.ds(side * toks, toks)]
        return remote(span, span, f_send.at[j, q], t_recv.at[j, side, q], peer(0, True))

    def route_arrivals(j, side):
        where = peer(0, True)
        return (
            remote(ids_in, ids.at[j, side], i_send.at[0, 1], i_recv.at[j, side], where),
            remote(probs_in, probs.at[j, side], p_send.at[0, 1], p_recv.at[j, side], where),
        )

    for d in range(chips):
        for other in (False, True):
            if d or other:
                for copy in route_copies(d, other):
                    copy.start()
    for q in range(parts):
        for d in range(1, chips):
            tok_copy(d, q).start()
        tok_copy(0, q).start()

    for q in range(parts):
        tok[0, q, pl.ds(0, toks), :] = tok_in[:, q * cq : (q + 1) * cq]

    local8 = scale.shape[0]
    earlier = jnp.where(
        lax.broadcasted_iota(jnp.int32, (toks, toks), 0)
        < lax.broadcasted_iota(jnp.int32, (toks, toks), 1),
        1.0, 0.0,
    ).astype(BF16)
    rid = lax.broadcasted_iota(jnp.int32, (slots, toks), 0).astype(F32)
    names = me * local + lax.broadcasted_iota(jnp.int32, (local8, toks), 0)
    step_now = step_in[0]

    def place(id_ref, prob_ref):
        member = jnp.zeros((local8, toks), F32)
        weight = jnp.zeros((local8, toks), F32)
        total = jnp.zeros((1, toks), F32)
        for k in range(topk):
            hit = id_ref[k] == names
            member = member + jnp.where(hit, 1.0, 0.0)
            weight = weight + jnp.where(hit, prob_ref[k], 0.0)
            total = total + prob_ref[k]
        count = jnp.dot(member.astype(BF16), earlier, preferred_element_type=F32)
        return jnp.where(member > 0.0, count, -4096.0), weight * (step_now / total)

    def tables(j, near, far):
        for e in range(local):
            low = rid == near[0][e : e + 1, :]
            high = (rid - cap) == far[0][e : e + 1, :]
            mmap[j, e * slots : (e + 1) * slots, :] = jnp.concatenate(
                [jnp.where(low, 1.0, 0.0), jnp.where(high, 1.0, 0.0)], axis=1
            ).astype(BF16)
            amount = jnp.sum(
                jnp.where(low, near[1][e : e + 1, :], 0.0)
                + jnp.where(high, far[1][e : e + 1, :], 0.0),
                axis=1, keepdims=True,
            )
            scale[e, pl.ds(pl.multiple_of(j * slots, 16), slots), :] = jnp.broadcast_to(
                amount, (slots, 128)
            )

    mine = place(ids_in, probs_in)
    for copy in route_arrivals(0, 1):
        copy.wait_recv()
    tables(0, mine, place(ids.at[0, 1], probs.at[0, 1]))

    def clear(e, carry):
        acc_g[e] = jnp.zeros(acc_g.shape[1:], F32)
        acc_u[e] = jnp.zeros(acc_u.shape[1:], F32)
        squares[e] = jnp.zeros(squares.shape[1:], F32)
        return carry

    lax.fori_loop(0, local, clear, 0)

    def far_tables(j, carry):
        for side in range(2):
            for copy in route_arrivals(j, side):
                copy.wait_recv()
        tables(j, place(ids.at[j, 0], probs.at[j, 0]), place(ids.at[j, 1], probs.at[j, 1]))
        return carry

    lax.fori_loop(1, chips, far_tables, 0)

    def pass_on(q):
        for j in range(1, chips):
            tok_arrival(j, 0, q).wait_recv()
            forward_copy(j, q).start()

    pass_on(0)

    def gather_step(q, carry):
        tok_arrival(0, 1, q).wait_recv()
        for j in range(1, chips):
            tok_arrival(j, 1, q).wait_recv()
        span = pl.ds(pl.multiple_of(q * cq, 128), cq)

        def per_expert(e, c2):
            for kind in range(2):
                up_copy(kind, e, q).wait()
            for j in range(chips):
                chosen = mmap[j, pl.ds(pl.multiple_of(e * slots, 16), slots), :]
                rows[j * slots : (j + 1) * slots, :] = jnp.dot(
                    chosen, tok[j, q], preferred_element_type=F32
                ).astype(BF16)
            sums = squares[e]
            for i in range(cq // 128):
                piece = rows[:, i * 128 : (i + 1) * 128].astype(F32)
                sums = sums + piece * piece
            squares[e] = sums
            for i in range(ff // ft):
                cols = pl.ds(i * ft, ft)
                acc_g[e, :, cols] += jnp.dot(
                    rows[...], wg[e, span, cols], preferred_element_type=F32
                )
                acc_u[e, :, cols] += jnp.dot(
                    rows[...], wu[e, span, cols], preferred_element_type=F32
                )

            @pl.when((e == local // 2) & (q < parts - 1))
            def _():
                pass_on(q + 1)

            return c2

        lax.fori_loop(0, local, per_expert, 0)
        return carry

    lax.fori_loop(0, parts, gather_step, 0)

    def activate(e, carry):
        mean = jnp.sum(squares[e], axis=1, keepdims=True) * (1.0 / width)
        root = lax.rsqrt(mean + 1e-06)
        amount = root * scale[e, :, 0:1]
        for i in range(ff // 128):
            cols = pl.ds(i * 128, 128)
            gate = acc_g[e, :, cols] * root
            hid[e, :, cols] = (
                gate / (1.0 + jnp.exp(-gate)) * (acc_u[e, :, cols] * amount)
            ).astype(BF16)
        return carry

    lax.fori_loop(0, local, activate, 0)

    for e in range(local):
        down_copy(e).wait()

    def pair_copy(j, k):
        return remote(
            px_out.at[j, k], px_in.at[j, k], px_send.at[j, k], px_recv.at[j, k], peer(0, True)
        )

    def back_copy(j, k):
        slot = chips - j
        return remote(
            y_out.at[j, k], y_in.at[slot, k], y_send.at[j, k], y_recv.at[slot, k], peer(j, False)
        )

    def rise_copy(k):
        return remote(
            z_out.at[k], z_in.at[k], z_send.at[k], z_recv.at[k], {"tm": lax.rem(now + 1, steps)}
        )

    def down(k):
        cols = pl.ds(pl.multiple_of(k * dc, 128), dc)
        for e in range(local):
            result = jnp.dot(hid[e], wd[e, :, cols], preferred_element_type=F32).astype(BF16)
            for j in range(chips):
                ycat[j, e * slots : (e + 1) * slots, :] = result[j * slots : (j + 1) * slots]
        for j in [*range(1, chips), 0]:
            share = lax.dot_general(
                mmap[j], ycat[j], (((0,), (0,)), ((), ())), preferred_element_type=F32
            )
            px_out[j, k] = share[toks:].astype(BF16)
            keep[j, k] = share[:toks]
            pair_copy(j, k).start()

    def send_back(k):
        for j in range(1, chips):
            pair_copy(j, k).wait_recv()
            y_out[j, k] = (keep[j, k] + px_in[j, k].astype(F32)).astype(BF16)
            back_copy(j, k).start()

    down(0)

    def step(k, carry):
        down(k)
        send_back(k - 1)
        return carry

    lax.fori_loop(1, chunks, step, 0)
    send_back(chunks - 1)

    def finish(k, carry):
        cols = pl.ds(pl.multiple_of(k * dc, 128), dc)
        pair_copy(0, k).wait_recv()
        total = keep[0, k] + px_in[0, k].astype(F32)
        for j in range(1, chips):
            back_copy(chips - j, k).wait_recv()
            total = total + y_in[j, k].astype(F32)
        keep[0, k] = total

        @pl.when(now > 0)
        def _():
            rise_copy(k).wait_recv()
            keep[0, k] = keep[0, k] + z_in[k].astype(F32)

        @pl.when(now < steps - 1)
        def _():
            z_out[k] = keep[0, k].astype(BF16)
            rise_copy(k).start()

        out_ref[:, cols] = keep[0, k]
        return carry

    lax.fori_loop(0, chunks, finish, 0)

    for d in range(chips):
        for other in (False, True):
            if d or other:
                for copy in route_copies(d, other):
                    copy.wait_send()
        for q in range(parts):
            tok_copy(d, q).wait_send()
            if d:
                forward_copy(d, q).wait_send()

    def drain(k, carry):
        for j in range(chips):
            pair_copy(j, k).wait_send()
            if j:
                back_copy(j, k).wait_send()

        @pl.when(now < steps - 1)
        def _():
            rise_copy(k).wait_send()

        return carry

    lax.fori_loop(0, chunks, drain, 0)


def shards(mesh, tokens, route_ids, route_probs, step_size, start_state, w_gate, w_up, w_down):
    toks, width = tokens.shape[1:]
    topk = route_ids.shape[2]
    local, _, ff = w_gate.shape
    group = mesh.shape["expert"]
    steps = mesh.shape["tm"]
    chips = group // 2
    cap = 3 * toks * topk // (2 * local * group)
    slots = -(-2 * cap // 16) * 16
    dc, cq = fit(width, DC), fit(width, COLS)
    chunks, parts = width // dc, width // cq
    local8 = -(-local // 8) * 8

    vmem = pl.BlockSpec(memory_space=pltpu.VMEM)
    smem = pl.BlockSpec(memory_space=pltpu.SMEM)
    hbm = pl.BlockSpec(memory_space=pl.ANY)
    dma = pltpu.SemaphoreType.DMA
    total = pl.pallas_call(
        functools.partial(kernel, (chips, steps, cap, slots)),
        out_shape=jax.ShapeDtypeStruct((toks, width), F32),
        in_specs=[vmem, vmem, vmem, smem, hbm, hbm, hbm],
        out_specs=vmem,
        scratch_shapes=[
            pltpu.VMEM((local, width, ff), BF16),
            pltpu.VMEM((local, width, ff), BF16),
            pltpu.VMEM((local, ff, width), BF16),
            pltpu.VMEM((chips, parts, 2 * toks, cq), BF16),
            pltpu.VMEM((chips, 2, topk, 1, toks), jnp.int32),
            pltpu.VMEM((chips, 2, topk, 1, toks), F32),
            pltpu.VMEM((local8, chips * slots, 128), F32),
            pltpu.VMEM((local, chips * slots, 128), F32),
            pltpu.VMEM((chips * slots, cq), BF16),
            pltpu.VMEM((local, chips * slots, ff), F32),
            pltpu.VMEM((local, chips * slots, ff), F32),
            pltpu.VMEM((local, chips * slots, ff), BF16),
            pltpu.VMEM((chips, local * slots, 2 * toks), BF16),
            pltpu.VMEM((chips, local * slots, dc), BF16),
            pltpu.VMEM((chips, chunks, toks, dc), F32),
            pltpu.VMEM((chips, chunks, toks, dc), BF16),
            pltpu.VMEM((chips, chunks, toks, dc), BF16),
            pltpu.VMEM((chips, chunks, toks, dc), BF16),
            pltpu.VMEM((chips, chunks, toks, dc), BF16),
            pltpu.VMEM((chunks, toks, dc), BF16),
            pltpu.VMEM((chunks, toks, dc), BF16),
            dma((2, local, parts)),
            dma((local,)),
            dma((chips, parts)),
            dma((chips, parts)),
            dma((chips, 2, parts)),
            dma((chips, 2)),
            dma((chips, 2)),
            dma((chips, 2)),
            dma((chips, 2)),
            dma((chips, chunks)),
            dma((chips, chunks)),
            dma((chips, chunks)),
            dma((chips, chunks)),
            dma((chunks,)),
            dma((chunks,)),
        ],
        compiler_params=pltpu.CompilerParams(
            collective_id=0, has_side_effects=True, vmem_limit_bytes=67_043_328
        ),
    )(
        tokens[0], jnp.transpose(route_ids, (2, 0, 1)), jnp.transpose(route_probs, (2, 0, 1)),
        step_size, w_gate, w_up, w_down,
    )
    return (start_state + total)[None]


def solution(mesh):
    return jax.shard_map(
        functools.partial(shards, mesh),
        mesh=mesh,
        in_specs=(
            P("tm", ("copies", "expert"), None),
            P("tm", ("copies", "expert"), None),
            P("tm", ("copies", "expert"), None),
            P(("copies", "tm")),
            P(("copies", "expert"), None),
            P("expert", None, None),
            P("expert", None, None),
            P("expert", None, None),
        ),
        out_specs=P("tm", ("copies", "expert"), None),
        check_vma=False,
    )
```

```python
import functools

import jax
import jax.numpy as jnp
from jax import lax
from jax.experimental import pallas as pl
from jax.experimental.pallas import tpu as pltpu
from jax.sharding import PartitionSpec as P

MESH = pl.DeviceIdType.MESH
BF16 = jnp.bfloat16
F32 = jnp.float32
COLS = 512
FT = 768
DC = 256


def fit(total, wanted):
    return wanted if total % wanted == 0 else total


def kernel(
    dims,
    tok_in, ids_in, probs_in, step_in, wg_hbm, wu_hbm, wd_hbm, out_ref,
    wg, wu, wd, tok, ids, probs, scale, squares, rows, acc_g, acc_u, hid, mmap, ycat,
    keep, px_out, px_in, y_out, y_in, z_out, z_in,
    up_sem, down_sem, t_send, f_send, t_recv, i_send, i_recv, p_send, p_recv,
    px_send, px_recv, y_send, y_recv, z_send, z_recv,
):
    chips, steps, cap, slots = dims
    local, width, ff = wg.shape
    toks = tok_in.shape[0]
    topk = ids_in.shape[0]
    parts, cq = tok.shape[1], tok.shape[3]
    chunks, dc = keep.shape[1], keep.shape[3]
    ft = fit(ff, FT)
    me = lax.axis_index("expert")
    now = lax.axis_index("tm")
    core = lax.rem(me, 2)
    chip = lax.div(me, 2)

    def peer(offset, other):
        own = (1 - core) if other else core
        return {"expert": lax.rem(chip + offset, chips) * 2 + own}

    def remote(src, dst, send, recv, where):
        return pltpu.make_async_remote_copy(
            src_ref=src, dst_ref=dst, send_sem=send, recv_sem=recv,
            device_id=where, device_id_type=MESH,
        )

    def up_copy(kind, e, q):
        src, dst = ((wg_hbm, wg), (wu_hbm, wu))[kind]
        span = pl.ds(pl.multiple_of(q * cq, 128), cq)
        return pltpu.make_async_copy(src.at[e, span], dst.at[e, span], up_sem.at[kind, e, q])

    def down_copy(e):
        return pltpu.make_async_copy(wd_hbm.at[e], wd.at[e], down_sem.at[e])

    for q in range(parts):
        for e in range(local):
            for kind in range(2):
                up_copy(kind, e, q).start()
    for e in range(local):
        down_copy(e).start()

    barrier = pltpu.get_barrier_semaphore()
    for d in range(chips):
        for other in (False, True):
            if d or other:
                pl.semaphore_signal(barrier, inc=1, device_id=peer(d, other), device_id_type=MESH)

    @pl.when(now > 0)
    def _():
        pl.semaphore_signal(barrier, inc=1, device_id={"tm": now - 1}, device_id_type=MESH)

    @pl.when(now < steps - 1)
    def _():
        pl.semaphore_signal(barrier, inc=1, device_id={"tm": now + 1}, device_id_type=MESH)

    peers = 2 * chips - 1 + jnp.where(now > 0, 1, 0) + jnp.where(now < steps - 1, 1, 0)
    pl.semaphore_wait(barrier, peers)

    def tok_copy(d, q):
        slot, side = ((chips - d) % chips, 0) if d else (0, 1)
        return remote(
            tok_in.at[:, pl.ds(q * cq, cq)], tok.at[slot, q, pl.ds(side * toks, toks)],
            t_send.at[d, q], t_recv.at[slot, side, q], peer(d, d == 0),
        )

    def route_copies(d, other):
        slot, side = (chips - d) % chips, int(other)
        where = peer(d, other)
        return (
            remote(ids_in, ids.at[slot, side], i_send.at[d, side], i_recv.at[slot, side], where),
            remote(
                probs_in, probs.at[slot, side], p_send.at[d, side], p_recv.at[slot, side], where
            ),
        )

    def forward_copy(j, q):
        return remote(
            tok.at[j, q, pl.ds(0, toks)], tok.at[j, q, pl.ds(toks, toks)],
            f_send.at[j, q], t_recv.at[j, 1, q], peer(0, True),
        )

    def tok_arrival(j, side, q):
        span = tok.at[j, q, pl.ds(side * toks, toks)]
        return remote(span, span, f_send.at[j, q], t_recv.at[j, side, q], peer(0, True))

    def route_arrivals(j, side):
        where = peer(0, True)
        return (
            remote(ids_in, ids.at[j, side], i_send.at[0, 1], i_recv.at[j, side], where),
            remote(probs_in, probs.at[j, side], p_send.at[0, 1], p_recv.at[j, side], where),
        )

    for d in range(chips):
        for other in (False, True):
            if d or other:
                for copy in route_copies(d, other):
                    copy.start()
    for q in range(parts):
        for d in range(1, chips):
            tok_copy(d, q).start()
        tok_copy(0, q).start()

    for q in range(parts):
        tok[0, q, pl.ds(0, toks), :] = tok_in[:, q * cq : (q + 1) * cq]

    local8 = scale.shape[0]
    earlier = jnp.where(
        lax.broadcasted_iota(jnp.int32, (toks, toks), 0)
        < lax.broadcasted_iota(jnp.int32, (toks, toks), 1),
        1.0, 0.0,
    ).astype(BF16)
    rid = lax.broadcasted_iota(jnp.int32, (slots, toks), 0).astype(F32)
    names = me * local + lax.broadcasted_iota(jnp.int32, (local8, toks), 0)
    step_now = step_in[0]

    def place(id_ref, prob_ref):
        member = jnp.zeros((local8, toks), F32)
        weight = jnp.zeros((local8, toks), F32)
        total = jnp.zeros((1, toks), F32)
        for k in range(topk):
            hit = id_ref[k] == names
            member = member + jnp.where(hit, 1.0, 0.0)
            weight = weight + jnp.where(hit, prob_ref[k], 0.0)
            total = total + prob_ref[k]
        count = jnp.dot(member.astype(BF16), earlier, preferred_element_type=F32)
        return jnp.where(member > 0.0, count, -4096.0), weight * (step_now / total)

    def tables(j, near, far):
        for e in range(local):
            low = rid == near[0][e : e + 1, :]
            high = (rid - cap) == far[0][e : e + 1, :]
            mmap[j, e * slots : (e + 1) * slots, :] = jnp.concatenate(
                [jnp.where(low, 1.0, 0.0), jnp.where(high, 1.0, 0.0)], axis=1
            ).astype(BF16)
            amount = jnp.sum(
                jnp.where(low, near[1][e : e + 1, :], 0.0)
                + jnp.where(high, far[1][e : e + 1, :], 0.0),
                axis=1, keepdims=True,
            )
            scale[e, pl.ds(pl.multiple_of(j * slots, 16), slots), :] = jnp.broadcast_to(
                amount, (slots, 128)
            )

    mine = place(ids_in, probs_in)
    for copy in route_arrivals(0, 1):
        copy.wait_recv()
    tables(0, mine, place(ids.at[0, 1], probs.at[0, 1]))

    def clear(e, carry):
        acc_g[e] = jnp.zeros(acc_g.shape[1:], F32)
        acc_u[e] = jnp.zeros(acc_u.shape[1:], F32)
        squares[e] = jnp.zeros(squares.shape[1:], F32)
        return carry

    lax.fori_loop(0, local, clear, 0)

    def far_tables(j, carry):
        for side in range(2):
            for copy in route_arrivals(j, side):
                copy.wait_recv()
        tables(j, place(ids.at[j, 0], probs.at[j, 0]), place(ids.at[j, 1], probs.at[j, 1]))
        return carry

    lax.fori_loop(1, chips, far_tables, 0)

    def pass_on(q):
        for j in range(1, chips):
            tok_arrival(j, 0, q).wait_recv()
            forward_copy(j, q).start()

    pass_on(0)

    def gather_step(q, carry):
        tok_arrival(0, 1, q).wait_recv()
        for j in range(1, chips):
            tok_arrival(j, 1, q).wait_recv()
        span = pl.ds(pl.multiple_of(q * cq, 128), cq)

        def per_expert(e, c2):
            for kind in range(2):
                up_copy(kind, e, q).wait()
            for j in range(chips):
                chosen = mmap[j, pl.ds(pl.multiple_of(e * slots, 16), slots), :]
                rows[j * slots : (j + 1) * slots, :] = jnp.dot(
                    chosen, tok[j, q], preferred_element_type=F32
                ).astype(BF16)
            sums = squares[e]
            for i in range(cq // 128):
                piece = rows[:, i * 128 : (i + 1) * 128].astype(F32)
                sums = sums + piece * piece
            squares[e] = sums
            for i in range(ff // ft):
                cols = pl.ds(i * ft, ft)
                acc_g[e, :, cols] += jnp.dot(
                    rows[...], wg[e, span, cols], preferred_element_type=F32
                )
                acc_u[e, :, cols] += jnp.dot(
                    rows[...], wu[e, span, cols], preferred_element_type=F32
                )

            @pl.when((e == local // 2) & (q < parts - 1))
            def _():
                pass_on(q + 1)

            return c2

        lax.fori_loop(0, local, per_expert, 0)
        return carry

    lax.fori_loop(0, parts, gather_step, 0)

    def activate(e, carry):
        mean = jnp.sum(squares[e], axis=1, keepdims=True) * (1.0 / width)
        root = lax.rsqrt(mean + 1e-06)
        amount = root * scale[e, :, 0:1]
        for i in range(ff // 128):
            cols = pl.ds(i * 128, 128)
            gate = acc_g[e, :, cols] * root
            hid[e, :, cols] = (
                gate / (1.0 + jnp.exp(-gate)) * (acc_u[e, :, cols] * amount)
            ).astype(BF16)
        return carry

    lax.fori_loop(0, local, activate, 0)

    for e in range(local):
        down_copy(e).wait()

    def pair_copy(j, k):
        return remote(
            px_out.at[j, k], px_in.at[j, k], px_send.at[j, k], px_recv.at[j, k], peer(0, True)
        )

    def back_copy(j, k):
        slot = chips - j
        return remote(
            y_out.at[j, k], y_in.at[slot, k], y_send.at[j, k], y_recv.at[slot, k], peer(j, False)
        )

    def rise_copy(k):
        return remote(
            z_out.at[k], z_in.at[k], z_send.at[k], z_recv.at[k], {"tm": lax.rem(now + 1, steps)}
        )

    def down(k):
        cols = pl.ds(pl.multiple_of(k * dc, 128), dc)
        for e in range(local):
            result = jnp.dot(hid[e], wd[e, :, cols], preferred_element_type=F32).astype(BF16)
            for j in range(chips):
                ycat[j, e * slots : (e + 1) * slots, :] = result[j * slots : (j + 1) * slots]
        for j in [*range(1, chips), 0]:
            share = lax.dot_general(
                mmap[j], ycat[j], (((0,), (0,)), ((), ())), preferred_element_type=F32
            )
            px_out[j, k] = share[toks:].astype(BF16)
            keep[j, k] = share[:toks]
            pair_copy(j, k).start()

    def send_back(k):
        for j in range(1, chips):
            pair_copy(j, k).wait_recv()
            y_out[j, k] = (keep[j, k] + px_in[j, k].astype(F32)).astype(BF16)
            back_copy(j, k).start()

    down(0)

    def step(k, carry):
        down(k)
        send_back(k - 1)
        return carry

    lax.fori_loop(1, chunks, step, 0)
    send_back(chunks - 1)

    def finish(k, carry):
        cols = pl.ds(pl.multiple_of(k * dc, 128), dc)
        pair_copy(0, k).wait_recv()
        total = keep[0, k] + px_in[0, k].astype(F32)
        for j in range(1, chips):
            back_copy(chips - j, k).wait_recv()
            total = total + y_in[j, k].astype(F32)
        keep[0, k] = total

        @pl.when(now > 0)
        def _():
            rise_copy(k).wait_recv()
            keep[0, k] = keep[0, k] + z_in[k].astype(F32)

        @pl.when(now < steps - 1)
        def _():
            z_out[k] = keep[0, k].astype(BF16)
            rise_copy(k).start()

        out_ref[:, cols] = keep[0, k]
        return carry

    lax.fori_loop(0, chunks, finish, 0)

    for d in range(chips):
        for other in (False, True):
            if d or other:
                for copy in route_copies(d, other):
                    copy.wait_send()
        for q in range(parts):
            tok_copy(d, q).wait_send()
            if d:
                forward_copy(d, q).wait_send()

    def drain(k, carry):
        for j in range(chips):
            pair_copy(j, k).wait_send()
            if j:
                back_copy(j, k).wait_send()

        @pl.when(now < steps - 1)
        def _():
            rise_copy(k).wait_send()

        return carry

    lax.fori_loop(0, chunks, drain, 0)


def shards(mesh, tokens, route_ids, route_probs, step_size, start_state, w_gate, w_up, w_down):
    toks, width = tokens.shape[1:]
    topk = route_ids.shape[2]
    local, _, ff = w_gate.shape
    group = mesh.shape["expert"]
    steps = mesh.shape["tm"]
    chips = group // 2
    cap = 3 * toks * topk // (2 * local * group)
    slots = -(-2 * cap // 16) * 16
    dc, cq = fit(width, DC), fit(width, COLS)
    chunks, parts = width // dc, width // cq
    local8 = -(-local // 8) * 8

    vmem = pl.BlockSpec(memory_space=pltpu.VMEM)
    smem = pl.BlockSpec(memory_space=pltpu.SMEM)
    hbm = pl.BlockSpec(memory_space=pl.ANY)
    dma = pltpu.SemaphoreType.DMA
    total = pl.pallas_call(
        functools.partial(kernel, (chips, steps, cap, slots)),
        out_shape=jax.ShapeDtypeStruct((toks, width), F32),
        in_specs=[vmem, vmem, vmem, smem, hbm, hbm, hbm],
        out_specs=vmem,
        scratch_shapes=[
            pltpu.VMEM((local, width, ff), BF16),
            pltpu.VMEM((local, width, ff), BF16),
            pltpu.VMEM((local, ff, width), BF16),
            pltpu.VMEM((chips, parts, 2 * toks, cq), BF16),
            pltpu.VMEM((chips, 2, topk, 1, toks), jnp.int32),
            pltpu.VMEM((chips, 2, topk, 1, toks), F32),
            pltpu.VMEM((local8, chips * slots, 128), F32),
            pltpu.VMEM((local, chips * slots, 128), F32),
            pltpu.VMEM((chips * slots, cq), BF16),
            pltpu.VMEM((local, chips * slots, ff), F32),
            pltpu.VMEM((local, chips * slots, ff), F32),
            pltpu.VMEM((local, chips * slots, ff), BF16),
            pltpu.VMEM((chips, local * slots, 2 * toks), BF16),
            pltpu.VMEM((chips, local * slots, dc), BF16),
            pltpu.VMEM((chips, chunks, toks, dc), F32),
            pltpu.VMEM((chips, chunks, toks, dc), BF16),
            pltpu.VMEM((chips, chunks, toks, dc), BF16),
            pltpu.VMEM((chips, chunks, toks, dc), BF16),
            pltpu.VMEM((chips, chunks, toks, dc), BF16),
            pltpu.VMEM((chunks, toks, dc), BF16),
            pltpu.VMEM((chunks, toks, dc), BF16),
            dma((2, local, parts)),
            dma((local,)),
            dma((chips, parts)),
            dma((chips, parts)),
            dma((chips, 2, parts)),
            dma((chips, 2)),
            dma((chips, 2)),
            dma((chips, 2)),
            dma((chips, 2)),
            dma((chips, chunks)),
            dma((chips, chunks)),
            dma((chips, chunks)),
            dma((chips, chunks)),
            dma((chunks,)),
            dma((chunks,)),
        ],
        compiler_params=pltpu.CompilerParams(
            collective_id=0, has_side_effects=True, vmem_limit_bytes=67_043_328
        ),
    )(
        tokens[0], jnp.transpose(route_ids, (2, 0, 1)), jnp.transpose(route_probs, (2, 0, 1)),
        step_size, w_gate, w_up, w_down,
    )
    return (start_state + total)[None]


def solution(mesh):
    return jax.shard_map(
        functools.partial(shards, mesh),
        mesh=mesh,
        in_specs=(
            P("tm", ("copies", "expert"), None),
            P("tm", ("copies", "expert"), None),
            P("tm", ("copies", "expert"), None),
            P(("copies", "tm")),
            P(("copies", "expert"), None),
            P("expert", None, None),
            P("expert", None, None),
            P("expert", None, None),
        ),
        out_specs=P("tm", ("copies", "expert"), None),
        check_vma=False,
    )
```
